128 devices in a mesh: child: 4 (over y), row: 4 (over x), col: 8 (over z, core).
Axes of the slice: x: 4, y: 4, z: 4, core: 2. Of those that a mesh axis runs over, the one named last changes fastest.
Arguments:
- parent_solution: float32 [16384, 256], P(('child', 'row', 'col')), may hold values from -6 to 6
- border_owner: int32 [4, 8192, 1], replicated, may hold values from 0 to 127; in each aligned block of 256 rows (0 to 255, 256 to 511, ..., all dimensions but the last counted through in order) at most 4 rows name the same one
- border_slot: int32 [4, 8192], replicated, may hold values from 0 to 127
- border_tile: float32 [4, 8192, 8192], P('child', 'row', 'col'), may hold values from -0.0625 to 0.0625
- pivot_inverse: float32 [4, 8192, 8192], P('child', 'row', 'col'), may hold values from -0.0625 to 0.0625
- pivot_rhs: float32 [4, 8192, 256], P('child', 'col'), may hold values from -6 to 6
Outputs:
- pivot_solution: float32 [4, 8192, 256], P('child', ('row', 'col'))
The draws below stay inside these ranges and needn't reach their ends.
Inputs may be any that keep to these rules, and one draw needn't show every extreme that they name: `border_owner`: within each aligned block of 256 border rows of one front, no device is named more than 4 times, and some device is named exactly 4 times in some blocks.
All inputs are finite; a program needn't handle non-finite values.
Results may differ from the reference program's by a relative error of at most 0.0003.
Values sent between devices are 32-bit elements; how exact they have to be, the bound alone decides.
No kernel may reach another device: no remote copies, remote signals or barrier semaphores. Data moves between devices by JAX's collectives and lax.ppermute only.
A program may use at most 128 MiB of HBM per device.

```python
import math
import jax
import jax.numpy as jnp
import numpy as np
from jax import lax

BD = 256
P_SIZE = 8192
LOADS = 256
NPD = 128
B = 8192
NPAR = 16384
CAP = 4
N_CHILD = 4
DEVICES = 128


def place_ends(array, rng, least, largest):
    index_at = [jax.random.randint(jax.random.fold_in(rng, axis), (), 0, length) for axis, length in enumerate(array.shape)]
    widest = array.shape.index(max(array.shape))
    next_to = index_at[:widest] + [(index_at[widest] + 1) % array.shape[widest]] + index_at[widest + 1:]
    return array.at[tuple(index_at)].set(least).at[tuple(next_to)].set(largest)


def block_scale(rng, extent, split, least, largest):
    def one(axis_at, parts):
        heights = jax.random.uniform(jax.random.fold_in(jax.random.fold_in(rng, 6), axis_at), (parts,), jnp.float32, least / len(split), largest / len(split))
        return jnp.repeat(jnp.exp(heights), extent[axis_at] // parts).reshape((-1,) + (1,) * (len(extent) - axis_at - 1))

    level = one(*split[0])
    for cut in split[1:]:
        level = level * one(*cut)
    return level


def deal_out(rng, own, number, rows, count, top, limit, slope):
    order = jax.random.permutation(rng, count)
    crowded, ordinary = load_shares(count, rows * top, limit, slope, True), load_shares(count, rows * top, limit, slope, False)
    places = jnp.arange(count)

    def named(lengths, turn):
        used = int((lengths > 0).sum())
        fixed = max(1, used // 4)
        shifted = fixed + (places - fixed + turn * (used - fixed)) % max(1, count - fixed)
        return jnp.zeros((count,), jnp.int32).at[order[jnp.where(places < fixed, places, shifted)]].set(jnp.asarray(lengths, jnp.int32))

    lengths = jnp.where(number % 4 == 0, named(crowded, number // 4), named(ordinary, number - number // 4 - 1))
    mixed = jax.random.permutation(jax.random.fold_in(own, 3), count)
    source_of, sink = mixed[0:count // 2 * 2:2], mixed[1:count // 2 * 2:2]
    margin = jnp.minimum(lengths[source_of] - 1, limit - lengths[sink]) // 2
    margin = jnp.where((source_of == order[0]) | (sink == order[0]) | (lengths[sink] == 0), 0, jnp.maximum(margin, 0))
    shifted = jax.random.randint(jax.random.fold_in(own, 4), (count // 2,), 0, 1 << 20) % (margin + 1)
    lengths = lengths.at[source_of].add(-shifted).at[sink].add(shifted)
    labels = jnp.searchsorted(jnp.cumsum(lengths), jnp.arange(rows * top), side="right").astype(jnp.int32)
    listing = labels.reshape(top, rows).T
    listing = listing[jax.random.permutation(jax.random.fold_in(own, 1), rows)]
    turn = jax.random.randint(jax.random.fold_in(own, 2), (rows, 1), 0, top)
    return jnp.take_along_axis(listing, (jnp.arange(top)[None, :] + turn) % top, axis=1)


def load_shares(amount, total, bound, slope, full):
    loads = [(1 << 20) // math.isqrt(grade ** slope) + 1 for grade in range(1, amount + 1)]
    largest = bound if full else min(bound, max(-(-total // amount), total * loads[0] // sum(loads)))
    least = 1 if total - largest >= amount - 1 else 0
    given, rest = [largest] + [least] * (amount - 1), total - largest - least * (amount - 1)
    while rest > 0:
        movable = [i for i in range(1, amount) if given[i] < largest] or [i for i in range(1, amount) if given[i] < bound]
        pool, remaining = sum([loads[i] for i in movable]), rest
        for i in movable:
            addition = min(bound - given[i], max(1, remaining * loads[i] // pool), rest)
            given[i] = given[i] + addition
            rest = rest - addition
    return np.array(given)


def normal_values(stream_key, shape, width, reach, split=(), dtype=jnp.bfloat16):
    entries = jax.random.normal(stream_key, shape, jnp.float32) * width
    if len(split) > 0:
        entries = block_scale(stream_key, shape, split, -0.22, 0.18) * entries
    return jnp.clip(entries, min=-reach, max=reach).astype(dtype)


def setup_inputs(seed: int = 0) -> dict:
    streams_of = jax.random.split(jax.random.key(seed), 7)
    parent_solution = normal_values(streams_of[0], (NPAR, LOADS), 1.0, 6.0, ((0, 128),), jnp.float32)
    border_owner_keys = jax.random.split(jax.random.fold_in(streams_of[1], 1), N_CHILD * B // BD)
    border_owner_turns = jax.random.permutation(jax.random.fold_in(streams_of[1], 3), N_CHILD * B // BD)
    border_owner = jax.vmap(lambda own, number: deal_out(jax.random.fold_in(streams_of[1], 2), own, number, BD, DEVICES, 1, CAP, 2))(border_owner_keys, border_owner_turns).reshape((N_CHILD, B, 1))
    border_slot = place_ends(jax.random.randint(streams_of[2], (N_CHILD, B), 0, NPD), jax.random.fold_in(streams_of[2], 1), 0, NPD - 1).astype(jnp.int32)
    border_tile = normal_values(streams_of[3], (N_CHILD, B, P_SIZE), B ** -0.5, 0.0625, ((0, 4), (1, 4), (2, 8)), jnp.float32)
    pivot_inverse = normal_values(streams_of[4], (N_CHILD, P_SIZE, P_SIZE), P_SIZE ** -0.5, 0.0625, ((0, 4), (1, 4), (2, 8)), jnp.float32)
    pivot_rhs = normal_values(streams_of[5], (N_CHILD, P_SIZE, LOADS), 1.0, 6.0, ((0, 4), (1, 8)), jnp.float32)
    return dict(parent_solution=parent_solution, border_owner=border_owner, border_slot=border_slot, border_tile=border_tile, pivot_inverse=pivot_inverse, pivot_rhs=pivot_rhs)


def reference(parent_solution, border_owner, border_slot, border_tile, pivot_inverse, pivot_rhs):
    parent_index = (border_owner[:, :, 0] * NPD + border_slot).astype(jnp.int32)
    results = []
    for front_number in range(N_CHILD):
        border_values = jnp.take(parent_solution, parent_index[front_number], axis=0)
        coupled = jnp.dot(border_tile[front_number].T, border_values, precision=lax.Precision.HIGHEST, preferred_element_type=jnp.float32)
        reduced = pivot_rhs[front_number] - coupled
        solved = jnp.dot(pivot_inverse[front_number], reduced, precision=lax.Precision.HIGHEST, preferred_element_type=jnp.float32)
        results.append(solved)
    return jnp.stack(results)
```

```python
import functools

import jax
import jax.numpy as jnp
from jax import lax
from jax.experimental import pallas as pl
from jax.experimental.pallas import tpu as pltpu
from jax.sharding import PartitionSpec as P

F32 = jnp.float32
BF16 = jnp.bfloat16
I32 = jnp.int32
SLOTS = 4


def dot(a, b):
    return jnp.dot(a, b, preferred_element_type=F32)


def split2(x):
    hi = x.astype(BF16)
    return hi, (x - hi.astype(F32)).astype(BF16)


def split3(x):
    hi = x.astype(BF16)
    rest = x - hi.astype(F32)
    mid = rest.astype(BF16)
    return hi, mid, (rest - mid.astype(F32)).astype(BF16)


def ones_upto(n):
    rows = lax.broadcasted_iota(I32, (n, n), 0)
    cols = lax.broadcasted_iota(I32, (n, n), 1)
    return jnp.where(rows <= cols, 1.0, 0.0).astype(BF16)


def indicator(flag):
    return jnp.where(flag, 1.0, 0.0).astype(BF16)


def pick_kernel(idx_ref, owner_ref, slot_ref, parent_ref, out_ref):
    me = idx_ref[0]
    blocks = owner_ref.shape[0] // 2
    lanes = owner_ref.shape[1]
    upto = ones_upto(lanes)
    parts = [split3(parent_ref[:, h * lanes:(h + 1) * lanes]) for h in range(2)]
    mask = [owner_ref[pl.ds(h, blocks, stride=2), :] == me for h in range(2)]
    slot = []
    children = 4
    per_child = blocks // children
    for h in range(2):
        slot.append(jnp.concatenate(
            [slot_ref[pl.ds(children * h + c, per_child, stride=2 * children), :]
             for c in range(children)], axis=0))
    count0 = dot(indicator(mask[0]), upto)
    count1 = dot(indicator(mask[1]), upto) + count0[:, lanes - 1:lanes]
    count = [count0, count1]
    local = lax.broadcasted_iota(I32, (blocks, lanes), 1)
    for p in range(SLOTS):
        asked = jnp.zeros((blocks, 1), I32)
        for h in range(2):
            chosen = mask[h] & (count[h] == float(p + 1))
            asked = asked + jnp.sum(jnp.where(chosen, slot[h] + 1, 0), axis=1, keepdims=True)
        select = indicator(local + 1 == asked)
        for h in range(2):
            hi, mid, lo = parts[h]
            out_ref[pl.ds(2 * p + h, blocks, stride=2 * SLOTS), :] = (
                dot(select, lo) + dot(select, mid)) + dot(select, hi)


def place_kernel(idx_ref, owner_ref, got_ref, out_ref):
    me = idx_ref[0]
    lanes = owner_ref.shape[1]
    devices = got_ref.shape[0] // (2 * SLOTS)
    upto = ones_upto(lanes)
    source = lax.broadcasted_iota(I32, (devices, lanes), 0)
    flag = [source == owner_ref[pl.ds(2 * me + h, 1), :] for h in range(2)]
    count0 = dot(indicator(flag[0]), upto)
    count1 = dot(indicator(flag[1]), upto) + count0[:, lanes - 1:lanes]
    count = [count0, count1]
    for half in range(2):
        acc = [jnp.zeros((lanes, lanes), F32) for _ in range(2)]
        for p in range(SLOTS):
            rows = got_ref[pl.ds(2 * p + half, devices, stride=2 * SLOTS), :]
            parts = split3(rows.T)
            for h in range(2):
                choose = indicator(flag[h] & (count[h] == float(p + 1)))
                for part in parts:
                    acc[h] = acc[h] + dot(part, choose)
        for h in range(2):
            out_ref[half * lanes:(half + 1) * lanes, h * lanes:(h + 1) * lanes] = acc[h]


def couple_kernel(idx_ref, values_ref, tile_ref, *outs):
    s = pl.program_id(0)
    blocks, loads, rows = values_ref.shape
    acc = None
    for b in range(blocks):
        vh, vl = split2(values_ref[b])
        th, tl = split2(tile_ref[b * rows:(b + 1) * rows, :])
        part = dot(vh, th) + (dot(vh, tl) + dot(vl, th))
        acc = part if acc is None else acc + part
    for i, out in enumerate(outs):
        @pl.when(s == i)
        def _(out=out):
            out[...] = acc


def reduce_kernel(idx_ref, rhs_ref, a_ref, b_ref, c_ref, d_ref, out_ref):
    total = (a_ref[...] + b_ref[...]) + (c_ref[...] + d_ref[...])
    out_ref[...] = rhs_ref[...] - total.T


def solve_kernel(idx_ref, inv_ref, a_ref, b_ref, c_ref, d_ref, out_ref):
    row = idx_ref[1]
    acc = None
    for s, ref in enumerate((a_ref, b_ref, c_ref, d_ref)):
        q = ref.shape[0]
        start = pl.multiple_of(((row + s) % 4) * q, q)
        ih, il = split2(inv_ref[:, pl.ds(start, q)])
        rh, rl = split2(ref[...])
        part = dot(ih, rh) + (dot(ih, rl) + dot(il, rh))
        acc = part if acc is None else acc + part
    out_ref[...] = acc


def shards(parent_solution, border_owner, border_slot, border_tile, pivot_inverse, pivot_rhs):
    axes = ("child", "row", "col")
    n_child = lax.axis_size("child")
    n_row = lax.axis_size("row")
    n_col = lax.axis_size("col")
    n_z = n_col // 2
    devices = n_child * n_row * n_col
    me = lax.axis_index(axes)
    my_row = lax.axis_index("row")
    my_col = lax.axis_index("col")
    idx = jnp.stack([me, my_row, my_col // 2, my_col % 2]).astype(I32)
    tile = border_tile[0]
    inverse = pivot_inverse[0]
    rhs = pivot_rhs[0]
    loads = parent_solution.shape[1]
    lanes = 128
    border = border_slot.shape[1]
    block = border // (n_row * n_col)
    quarter = rhs.shape[0] // n_row
    owner = border_owner.reshape(n_child * border // lanes, lanes)
    slot = border_slot.reshape(n_child, border // lanes, lanes).transpose(1, 0, 2).reshape(
        n_child * border // lanes, lanes)

    smem = pl.BlockSpec(memory_space=pltpu.SMEM)
    vmem = pl.BlockSpec(memory_space=pltpu.VMEM)
    params = functools.partial(pltpu.CompilerParams, vmem_limit_bytes=48 << 20)

    outgoing = pl.pallas_call(
        pick_kernel,
        in_specs=[smem, vmem, vmem, vmem],
        out_specs=vmem,
        out_shape=jax.ShapeDtypeStruct((devices * 2 * SLOTS, lanes), F32),
        compiler_params=params(),
        name="pick",
    )(idx, owner, slot, parent_solution)
    received = lax.all_to_all(
        outgoing.reshape(devices, 2 * SLOTS, lanes), axes, split_axis=0, concat_axis=0, tiled=True)
    placed = pl.pallas_call(
        place_kernel,
        in_specs=[smem, vmem, vmem],
        out_specs=vmem,
        out_shape=jax.ShapeDtypeStruct((loads, block), F32),
        compiler_params=params(),
        name="place",
    )(idx, owner, received.reshape(devices * 2 * SLOTS, lanes))
    values = lax.all_gather(placed, "col", axis=0, tiled=False)

    square = jax.ShapeDtypeStruct((loads, quarter), F32)
    coupled = pl.pallas_call(
        couple_kernel,
        grid_spec=pltpu.PrefetchScalarGridSpec(
            num_scalar_prefetch=1,
            grid=(n_row,),
            in_specs=[
                pl.BlockSpec(values.shape, lambda s, i: (0, 0, 0)),
                pl.BlockSpec((tile.shape[0], quarter), lambda s, i: (0, (i[1] + 2 + s) % 4)),
            ],
            out_specs=[pl.BlockSpec((loads, quarter), lambda s, i: (0, 0))] * n_row,
        ),
        out_shape=[square] * n_row,
        compiler_params=params(dimension_semantics=("arbitrary",)),
        name="couple",
    )(idx, values, tile)

    def shift(x, axis, by):
        n = lax.axis_size(axis)
        return lax.ppermute(x, axis, [(i, (i + by) % n) for i in range(n)])

    arrived = [shift(coupled[(s + 2) % 4], "row", s) for s in (2, 1, 3)]
    reduced = pl.pallas_call(
        reduce_kernel,
        grid_spec=pltpu.PrefetchScalarGridSpec(
            num_scalar_prefetch=1,
            grid=(1,),
            in_specs=[pl.BlockSpec((quarter, loads), lambda s, i: (i[1], 0))]
            + [pl.BlockSpec((loads, quarter), lambda s, i: (0, 0))] * 4,
            out_specs=pl.BlockSpec((quarter, loads), lambda s, i: (0, 0)),
        ),
        out_shape=jax.ShapeDtypeStruct((quarter, loads), F32),
        compiler_params=params(dimension_semantics=("arbitrary",)),
        name="reduce",
    )(idx, rhs, coupled[2], *arrived)
    far, near, back = [shift(reduced, "row", n_row - s) for s in (2, 1, 3)]
    pieces = [reduced, near, far, back]

    def solve(parity):
        return pl.pallas_call(
            solve_kernel,
            grid_spec=pltpu.PrefetchScalarGridSpec(
                num_scalar_prefetch=1,
                grid=(n_z,),
                in_specs=[pl.BlockSpec(
                    (block, inverse.shape[1]),
                    lambda s, i: (2 * ((i[2] + s) % 4) + (i[3] + parity) % 2, 0))]
                + [pl.BlockSpec((quarter, loads), lambda s, i: (0, 0))] * 4,
                out_specs=pl.BlockSpec((None, block, loads), lambda s, i: (s, 0, 0)),
            ),
            out_shape=jax.ShapeDtypeStruct((n_z, block, loads), F32),
            compiler_params=params(dimension_semantics=("arbitrary",)),
            name="solve",
        )(idx, inverse, *pieces)

    other = solve(1)
    swapped = lax.ppermute(other, "col", [(i, i ^ 1) for i in range(n_col)])
    mine = solve(0)
    chip = [mine[s] + swapped[s] for s in range(n_z)]

    def shift_z(x, by):
        return lax.ppermute(
            x, "col", [(2 * z + c, 2 * ((z + by) % n_z) + c) for z in range(n_z) for c in range(2)])

    got = [shift_z(chip[s], s) for s in (2, 1, 3)]
    return ((chip[0] + got[0]) + (got[1] + got[2]))[None]


def solution(mesh):
    return jax.shard_map(
        shards,
        mesh=mesh,
        in_specs=(
            P(("child", "row", "col"), None),
            P(),
            P(),
            P("child", "row", "col"),
            P("child", "row", "col"),
            P("child", "col", None),
        ),
        out_specs=P("child", ("row", "col"), None),
        check_vma=False,
    )
```

```python
import functools

import jax
import jax.numpy as jnp
from jax import lax
from jax.experimental import pallas as pl
from jax.experimental.pallas import tpu as pltpu
from jax.sharding import PartitionSpec as P

F32 = jnp.float32
BF16 = jnp.bfloat16
I32 = jnp.int32
CHUNKS = 2
SLOTS = 4


def position():
    col = lax.axis_index("col")
    return lax.axis_index(("child", "row", "col")), lax.axis_index("row"), col // 2, col % 2


def dot(a, b):
    return jnp.dot(a, b, preferred_element_type=F32)


def split2(x):
    hi = x.astype(BF16)
    return hi, (x - hi.astype(F32)).astype(BF16)


def split3(x):
    hi = x.astype(BF16)
    rest = x - hi.astype(F32)
    mid = rest.astype(BF16)
    return hi, mid, (rest - mid.astype(F32)).astype(BF16)


def ones_upto(n):
    rows = lax.broadcasted_iota(I32, (n, n), 0)
    cols = lax.broadcasted_iota(I32, (n, n), 1)
    return jnp.where(rows <= cols, 1.0, 0.0).astype(BF16)


def indicator(flag):
    return jnp.where(flag, 1.0, 0.0).astype(BF16)


def pick_kernel(owner_hbm, slot_hbm, parent_hbm, out_ref, mine_ref,
                owner_ref, slot_ref, parent_ref, sems):
    copies = [pltpu.make_async_copy(src, dst, sems.at[n]) for n, (src, dst) in enumerate(
        [(owner_hbm, owner_ref), (slot_hbm, slot_ref), (parent_hbm, parent_ref)])]
    for copy in copies:
        copy.start()
    copies[0].wait()
    me = position()[0]
    mine_ref[...] = owner_ref[pl.ds(2 * me, 2), :]
    blocks = owner_ref.shape[0] // 2
    lanes = owner_ref.shape[1]
    upto = ones_upto(lanes)
    copies[1].wait()
    copies[2].wait()
    parts = [split3(parent_ref[:, h * lanes:(h + 1) * lanes]) for h in range(2)]
    mask = [owner_ref[pl.ds(h, blocks, stride=2), :] == me for h in range(2)]
    slot = []
    children = 4
    per_child = blocks // children
    for h in range(2):
        slot.append(jnp.concatenate(
            [slot_ref[pl.ds(children * h + c, per_child, stride=2 * children), :]
             for c in range(children)], axis=0))
    count0 = dot(indicator(mask[0]), upto)
    count1 = dot(indicator(mask[1]), upto) + count0[:, lanes - 1:lanes]
    count = [count0, count1]
    local = lax.broadcasted_iota(I32, (blocks, lanes), 1)
    for p in range(SLOTS):
        asked = jnp.zeros((blocks, 1), I32)
        for h in range(2):
            chosen = mask[h] & (count[h] == float(p + 1))
            asked = asked + jnp.sum(jnp.where(chosen, slot[h] + 1, 0), axis=1, keepdims=True)
        select = indicator(local + 1 == asked)
        for h in range(2):
            hi, mid, lo = parts[h]
            out_ref[pl.ds(2 * p + h, blocks, stride=2 * SLOTS), :] = (
                dot(select, lo) + dot(select, mid)) + dot(select, hi)


def load_kernel(order_ref, tile_hbm, tile_ref, done_ref, sems):
    del order_ref
    done_ref[...] = jnp.zeros(done_ref.shape, F32)
    parts = sems.shape[0]
    rows = tile_ref.shape[0] // parts
    copies = []
    for n in range(parts):
        part = pl.ds(n * rows, rows)
        copies.append(pltpu.make_async_copy(tile_hbm.at[part], tile_ref.at[part], sems.at[n]))
    for copy in copies:
        copy.start()
    for copy in copies:
        copy.wait()


def place_kernel(mine_ref, got_ref, *refs, half):
    out_ref = refs[-1]
    lanes = mine_ref.shape[1]
    devices = got_ref.shape[0] // (2 * SLOTS)
    upto = ones_upto(lanes)
    source = lax.broadcasted_iota(I32, (devices, lanes), 0)
    flag = [source == mine_ref[h:h + 1, :] for h in range(2)]
    count0 = dot(indicator(flag[0]), upto)
    count1 = dot(indicator(flag[1]), upto) + count0[:, lanes - 1:lanes]
    count = [count0, count1]
    acc = [jnp.zeros((lanes, lanes), F32) for _ in range(2)]
    for p in range(SLOTS):
        rows = got_ref[pl.ds(2 * p + half, devices, stride=2 * SLOTS), :]
        parts = split3(rows.T)
        for h in range(2):
            choose = indicator(flag[h] & (count[h] == float(p + 1)))
            for part in parts:
                acc[h] = acc[h] + dot(part, choose)
    for h in range(2):
        out_ref[:, h * lanes:(h + 1) * lanes] = acc[h]


def stack_kernel(a_ref, b_ref, c_ref, d_ref, order_ref, out_ref):
    del order_ref
    for n, ref in enumerate((a_ref, b_ref, c_ref, d_ref)):
        out_ref[n] = ref[...]


def couple_kernel(tile_ref, *refs):
    values, outs, split_ref = refs[:-5], refs[-5:-1], refs[-1]
    _, row, z, core = position()
    for n in range(8):
        value = values[n % 2][n // 2]
        width, rows = value.shape
        block = 2 * ((z + 4 - n // 2) % 4) + (core + n % 2) % 2
        start = pl.multiple_of(block * rows, rows)
        vh, vl = split2(value)
        split_ref[:width, pl.ds(start, rows)] = vh
        split_ref[width:, pl.ds(start, rows)] = vl
    for s, out in enumerate(outs):
        cols = out.shape[1]
        start = pl.multiple_of(((row + 2 + s) % 4) * cols, cols)
        th, tl = split2(tile_ref[:, pl.ds(start, cols)])
        both = dot(split_ref[...], th)
        out[...] = both[:width] + (both[width:] + dot(split_ref[:width], tl))


def reduce_kernel(rhs_ref, a_ref, b_ref, c_ref, d_ref, out_ref, *, chunk):
    rows, width = out_ref.shape
    start = pl.multiple_of(position()[1] * rows, rows)
    total = (a_ref[...] + b_ref[...]) + (c_ref[...] + d_ref[...])
    out_ref[...] = rhs_ref[pl.ds(start, rows), chunk * width:(chunk + 1) * width] - total.T


def product(inv_ref, split_ref, parity, s):
    rows, width = 256, split_ref.shape[1] // 2
    _, _, z, core = position()
    start = pl.multiple_of((2 * ((z + 2 + s) % 4) + (core + parity) % 2) * rows, rows)
    ih, il = split2(inv_ref[pl.ds(start, rows), :])
    both = dot(ih, split_ref[...])
    return both[:, :width] + (both[:, width:] + dot(il, split_ref[:, :width]))


def split_pieces(refs, split_ref):
    row = position()[1]
    for s, ref in enumerate(refs):
        q, width = ref.shape
        start = pl.multiple_of(((row + s) % 4) * q, q)
        rh, rl = split2(ref[...])
        split_ref[pl.ds(start, q), :width] = rh
        split_ref[pl.ds(start, q), width:] = rl


def send_kernel(inv_ref, a_ref, b_ref, c_ref, d_ref, out_ref, split_ref):
    split_pieces((a_ref, b_ref, c_ref, d_ref), split_ref)
    for s in range(4):
        out_ref[s] = product(inv_ref, split_ref, 1, s)


def keep_kernel(inv_ref, a_ref, b_ref, c_ref, d_ref, add_ref, *rest):
    outs, split_ref = rest[:-1], rest[-1]
    split_pieces((a_ref, b_ref, c_ref, d_ref), split_ref)
    for s, out in enumerate(outs):
        out[...] = product(inv_ref, split_ref, 0, s) + add_ref[s]


def shards(parent_solution, border_owner, border_slot, border_tile, pivot_inverse, pivot_rhs):
    axes = ("child", "row", "col")
    n_child = lax.axis_size("child")
    n_row = lax.axis_size("row")
    n_col = lax.axis_size("col")
    n_z = n_col // 2
    devices = n_child * n_row * n_col
    rhs = pivot_rhs[0]
    loads = parent_solution.shape[1]
    lanes = 128
    width = loads // CHUNKS
    border = border_slot.shape[1]
    block = border // (n_row * n_col)
    quarter = rhs.shape[0] // n_row
    owner = border_owner.reshape(n_child * border // lanes, lanes)
    slot = border_slot.reshape(n_child, border // lanes, lanes).transpose(1, 0, 2).reshape(
        n_child * border // lanes, lanes)
    def arr(*shape):
        return jax.ShapeDtypeStruct(shape, F32)

    def shift(x, by):
        return lax.ppermute(x, "row", [(i, (i + by) % n_row) for i in range(n_row)])

    def shift_z(x, by):
        return lax.ppermute(
            x, "col", [(2 * z + c, 2 * ((z + by) % n_z) + c) for z in range(n_z) for c in range(2)])

    def swap(x):
        return lax.ppermute(x, "col", [(i, i ^ 1) for i in range(n_col)])

    dma = pltpu.SemaphoreType.DMA
    vmem = pl.BlockSpec(memory_space=pltpu.VMEM)
    hbm = pl.BlockSpec(memory_space=pltpu.HBM)
    anywhere = pl.BlockSpec(memory_space=pl.ANY)

    def in_hbm(x):
        return pltpu.with_memory_space_constraint(x, pltpu.HBM)

    def in_vmem(x):
        return pltpu.with_memory_space_constraint(x, pltpu.VMEM)

    outgoing, mine = pl.pallas_call(
        pick_kernel,
        in_specs=[hbm, hbm, hbm],
        out_specs=[vmem, vmem],
        out_shape=[arr(devices * 2 * SLOTS, lanes), jax.ShapeDtypeStruct((2, lanes), I32)],
        scratch_shapes=[pltpu.VMEM(owner.shape, I32), pltpu.VMEM(slot.shape, I32),
                        pltpu.VMEM(parent_solution.shape, F32), dma((3,))],
        compiler_params=pltpu.CompilerParams(vmem_limit_bytes=8 << 20),
        name="pick",
    )(in_hbm(owner), in_hbm(slot), in_hbm(parent_solution))
    received = lax.all_to_all(
        outgoing.reshape(devices, 2 * SLOTS, lanes), axes, split_axis=0, concat_axis=0, tiled=True)
    received = received.reshape(devices * 2 * SLOTS, lanes)
    inverse = pivot_inverse[0]
    def place(half, *order):
        return pl.pallas_call(
            functools.partial(place_kernel, half=half),
            in_specs=[vmem, vmem] + [anywhere] * len(order),
            out_specs=vmem,
            out_shape=arr(width, block),
            compiler_params=pltpu.CompilerParams(vmem_limit_bytes=8 << 20),
            name="place",
        )(mine, received, *order)

    first = place(0)
    tile, loaded = pl.pallas_call(
        load_kernel,
        in_specs=[anywhere, hbm],
        out_specs=[vmem, vmem],
        out_shape=[pltpu.VMEM(border_tile.shape[1:], F32), arr(8, lanes)],
        scratch_shapes=[dma((4,))],
        compiler_params=pltpu.CompilerParams(vmem_limit_bytes=4 << 20),
        cost_estimate=pl.CostEstimate(
            flops=0, transcendentals=0, bytes_accessed=8 * border_tile.shape[1] * border_tile.shape[2]),
        name="load",
    )(first, in_hbm(border_tile[0]))
    placed = [first, place(1, loaded)]

    def send_z(own):
        return {s: shift_z(own, s) for s in (2, 1, 3)}

    def gather(own, got, order):
        stacked = pl.pallas_call(
            stack_kernel,
            in_specs=[vmem] * n_z + [anywhere],
            out_specs=vmem,
            out_shape=arr(n_z, width, block),
            compiler_params=pltpu.CompilerParams(vmem_limit_bytes=4 << 20),
            name="stack",
        )(own, got[1], got[2], got[3], order)
        return [stacked, swap(stacked)]

    def held(kernel, name, scratch, out_shape, *args):
        return pl.pallas_call(
            kernel,
            in_specs=[vmem] * len(args),
            out_specs=jax.tree.map(lambda _: vmem, out_shape),
            out_shape=out_shape,
            scratch_shapes=scratch,
            compiler_params=pltpu.CompilerParams(vmem_limit_bytes=8 << 20),
            name=name,
        )(*args)

    def couple(values):
        return held(couple_kernel, "couple", [pltpu.VMEM((2 * width, tile.shape[0]), BF16)],
                    [arr(width, quarter)] * n_row, in_vmem(tile), *values)

    def reduce(coupled, chunk):
        arrived = [shift(coupled[(s + 2) % 4], s) for s in (2, 1, 3)]
        return held(functools.partial(reduce_kernel, chunk=chunk), "reduce", [],
                    arr(quarter, width), rhs, coupled[2], *arrived)

    def spread(reduced):
        far, near, back = [shift(reduced, n_row - s) for s in (2, 1, 3)]
        return [reduced, near, far, back]

    def solve(pieces):
        scratch = [pltpu.VMEM((inverse.shape[1], 2 * width), BF16)]
        other = held(send_kernel, "send", scratch, arr(n_z, block, width), inverse, *pieces)
        return held(keep_kernel, "keep", scratch, [arr(block, width)] * n_z,
                    inverse, *pieces, swap(other))

    def finish(chip):
        got = [shift_z(chip[(s + 2) % 4], s) for s in (2, 1, 3)]
        return (chip[2] + got[0]) + (got[1] + got[2])

    chunks = range(CHUNKS)
    sent = [send_z(placed[c]) for c in chunks]
    coupled = [couple(gather(placed[0], sent[0], placed[1]))]
    coupled.append(couple(gather(placed[1], sent[1], coupled[0][0])))
    reduced = [reduce(coupled[c], c) for c in chunks]
    pieces = [spread(reduced[c]) for c in chunks]
    chip = [solve(pieces[c]) for c in chunks]
    return jnp.concatenate([finish(chip[c]) for c in chunks], axis=1)[None]


def solution(mesh):
    return jax.shard_map(
        shards,
        mesh=mesh,
        in_specs=(
            P(("child", "row", "col"), None),
            P(),
            P(),
            P("child", "row", "col"),
            P("child", "row", "col"),
            P("child", "col", None),
        ),
        out_specs=P("child", ("row", "col"), None),
        check_vma=False,
    )
```

```python
import functools

import jax
import jax.numpy as jnp
from jax import lax
from jax.experimental import pallas as pl
from jax.experimental.pallas import tpu as pltpu
from jax.sharding import PartitionSpec as P

F32 = jnp.float32
BF16 = jnp.bfloat16
I32 = jnp.int32
CHUNKS = 2
SLOTS = 4


def position():
    col = lax.axis_index("col")
    return lax.axis_index(("child", "row", "col")), lax.axis_index("row"), col // 2, col % 2


def dot(a, b):
    return jnp.dot(a, b, preferred_element_type=F32)


def split2(x):
    hi = x.astype(BF16)
    return hi, (x - hi.astype(F32)).astype(BF16)


def split3(x):
    hi = x.astype(BF16)
    rest = x - hi.astype(F32)
    mid = rest.astype(BF16)
    return hi, mid, (rest - mid.astype(F32)).astype(BF16)


def ones_upto(n):
    rows = lax.broadcasted_iota(I32, (n, n), 0)
    cols = lax.broadcasted_iota(I32, (n, n), 1)
    return jnp.where(rows <= cols, 1.0, 0.0).astype(BF16)


def indicator(flag):
    return jnp.where(flag, 1.0, 0.0).astype(BF16)


def pick_kernel(owner_hbm, slot_hbm, parent_hbm, out_ref, mine_ref,
                owner_ref, slot_ref, parent_ref, sems):
    copies = [pltpu.make_async_copy(src, dst, sems.at[n]) for n, (src, dst) in enumerate(
        [(owner_hbm, owner_ref), (slot_hbm, slot_ref), (parent_hbm, parent_ref)])]
    for copy in copies:
        copy.start()
    copies[0].wait()
    me = position()[0]
    mine_ref[...] = owner_ref[pl.ds(2 * me, 2), :]
    blocks = owner_ref.shape[0] // 2
    lanes = owner_ref.shape[1]
    upto = ones_upto(lanes)
    copies[1].wait()
    copies[2].wait()
    parts = [split3(parent_ref[:, h * lanes:(h + 1) * lanes]) for h in range(2)]
    mask = [owner_ref[pl.ds(h, blocks, stride=2), :] == me for h in range(2)]
    slot = []
    children = 4
    per_child = blocks // children
    for h in range(2):
        slot.append(jnp.concatenate(
            [slot_ref[pl.ds(children * h + c, per_child, stride=2 * children), :]
             for c in range(children)], axis=0))
    count0 = dot(indicator(mask[0]), upto)
    count1 = dot(indicator(mask[1]), upto) + count0[:, lanes - 1:lanes]
    count = [count0, count1]
    local = lax.broadcasted_iota(I32, (blocks, lanes), 1)
    for p in range(SLOTS):
        asked = jnp.zeros((blocks, 1), I32)
        for h in range(2):
            chosen = mask[h] & (count[h] == float(p + 1))
            asked = asked + jnp.sum(jnp.where(chosen, slot[h] + 1, 0), axis=1, keepdims=True)
        select = indicator(local + 1 == asked)
        for h in range(2):
            hi, mid, lo = parts[h]
            out_ref[pl.ds(2 * p + h, blocks, stride=2 * SLOTS), :] = (
                dot(select, lo) + dot(select, mid)) + dot(select, hi)


def load_kernel(order_ref, tile_hbm, tile_ref, done_ref, sems):
    del order_ref
    done_ref[...] = jnp.zeros(done_ref.shape, F32)
    parts = sems.shape[0]
    rows = tile_ref.shape[0] // parts
    copies = []
    for n in range(parts):
        part = pl.ds(n * rows, rows)
        copies.append(pltpu.make_async_copy(tile_hbm.at[part], tile_ref.at[part], sems.at[n]))
    for copy in copies:
        copy.start()
    for copy in copies:
        copy.wait()


def place_kernel(mine_ref, got_ref, out_ref):
    lanes = mine_ref.shape[1]
    devices = got_ref.shape[0] // (2 * SLOTS)
    upto = ones_upto(lanes)
    source = lax.broadcasted_iota(I32, (devices, lanes), 0)
    flag = [source == mine_ref[h:h + 1, :] for h in range(2)]
    count0 = dot(indicator(flag[0]), upto)
    count1 = dot(indicator(flag[1]), upto) + count0[:, lanes - 1:lanes]
    count = [count0, count1]
    for half in range(2):
        acc = [jnp.zeros((lanes, lanes), F32) for _ in range(2)]
        for p in range(SLOTS):
            rows = got_ref[pl.ds(2 * p + half, devices, stride=2 * SLOTS), :]
            parts = split3(rows.T)
            for h in range(2):
                choose = indicator(flag[h] & (count[h] == float(p + 1)))
                for part in parts:
                    acc[h] = acc[h] + dot(part, choose)
        for h in range(2):
            out_ref[half * lanes:(half + 1) * lanes, h * lanes:(h + 1) * lanes] = acc[h]


def stack_kernel(a_ref, b_ref, c_ref, d_ref, order_ref, *outs):
    del order_ref
    width = outs[0].shape[1]
    for n, ref in enumerate((a_ref, b_ref, c_ref, d_ref)):
        for chunk, out in enumerate(outs):
            out[n] = ref[chunk * width:(chunk + 1) * width, :]


def block_rows(tile_ref, parity, first, cols, rows):
    _, _, z, core = position()
    parts = []
    for s in range(4):
        start = pl.multiple_of((2 * ((z + 4 - s) % 4) + (core + parity) % 2) * rows, rows)
        parts.append(tile_ref[pl.ds(start, rows), pl.ds(first, cols)])
    return jnp.concatenate(parts, axis=0)


def split_values(ref, split_ref, top, loads):
    n, width, rows = ref.shape
    for s in range(n):
        vh, vl = split2(ref[s])
        split_ref[top:top + width, s * rows:(s + 1) * rows] = vh
        split_ref[loads + top:loads + top + width, s * rows:(s + 1) * rows] = vl


def begin_kernel(tile_ref, a_ref, b_ref, out_ref, split_ref):
    width, rows = a_ref.shape[1:]
    loads = 2 * width
    split_values(a_ref, split_ref, 0, loads)
    split_values(b_ref, split_ref, width, loads)
    cols = out_ref.shape[2]
    for q in range(out_ref.shape[0]):
        th, tl = split2(block_rows(tile_ref, 0, q * cols, cols, rows))
        both = dot(split_ref[...], th)
        out_ref[q] = both[:loads] + (both[loads:] + dot(split_ref[:loads], tl))


def couple_kernel(tile_ref, sum_ref, other_ref, *rest, chunk):
    outs, split_ref = rest[:-1], rest[-1]
    row = position()[1]
    width, cols = outs[0].shape
    rows = other_ref.shape[2]
    split_values(other_ref, split_ref, 0, width)
    for s, out in enumerate(outs):
        q = (row + 2 + s) % 4
        th, tl = split2(block_rows(tile_ref, 1, pl.multiple_of(q * cols, cols), cols, rows))
        both = dot(split_ref[...], th)
        out[...] = sum_ref[q, chunk * width:(chunk + 1) * width, :] + (
            both[:width] + (both[width:] + dot(split_ref[:width], tl)))


def reduce_kernel(rhs_ref, a_ref, b_ref, c_ref, d_ref, out_ref, *, chunk):
    rows, width = out_ref.shape
    start = pl.multiple_of(position()[1] * rows, rows)
    total = (a_ref[...] + b_ref[...]) + (c_ref[...] + d_ref[...])
    out_ref[...] = rhs_ref[pl.ds(start, rows), chunk * width:(chunk + 1) * width] - total.T


def product(inv_ref, split_ref, parity, s):
    rows, width = 256, split_ref.shape[1] // 2
    _, _, z, core = position()
    start = pl.multiple_of((2 * ((z + 2 + s) % 4) + (core + parity) % 2) * rows, rows)
    ih, il = split2(inv_ref[pl.ds(start, rows), :])
    both = dot(ih, split_ref[...])
    return both[:, :width] + (both[:, width:] + dot(il, split_ref[:, :width]))


def split_pieces(refs, split_ref):
    row = position()[1]
    for s, ref in enumerate(refs):
        q, width = ref.shape
        start = pl.multiple_of(((row + s) % 4) * q, q)
        rh, rl = split2(ref[...])
        split_ref[pl.ds(start, q), :width] = rh
        split_ref[pl.ds(start, q), width:] = rl


def send_kernel(inv_ref, a_ref, b_ref, c_ref, d_ref, out_ref, split_ref):
    split_pieces((a_ref, b_ref, c_ref, d_ref), split_ref)
    for s in range(4):
        out_ref[s] = product(inv_ref, split_ref, 1, s)


def keep_kernel(inv_ref, a_ref, b_ref, c_ref, d_ref, add_ref, *rest):
    outs, split_ref = rest[:-1], rest[-1]
    split_pieces((a_ref, b_ref, c_ref, d_ref), split_ref)
    for s, out in enumerate(outs):
        out[...] = product(inv_ref, split_ref, 0, s) + add_ref[s]


def shards(parent_solution, border_owner, border_slot, border_tile, pivot_inverse, pivot_rhs):
    axes = ("child", "row", "col")
    n_child = lax.axis_size("child")
    n_row = lax.axis_size("row")
    n_col = lax.axis_size("col")
    n_z = n_col // 2
    devices = n_child * n_row * n_col
    rhs = pivot_rhs[0]
    loads = parent_solution.shape[1]
    lanes = 128
    width = loads // CHUNKS
    border = border_slot.shape[1]
    block = border // (n_row * n_col)
    quarter = rhs.shape[0] // n_row
    owner = border_owner.reshape(n_child * border // lanes, lanes)
    slot = border_slot.reshape(n_child, border // lanes, lanes).transpose(1, 0, 2).reshape(
        n_child * border // lanes, lanes)
    def arr(*shape):
        return jax.ShapeDtypeStruct(shape, F32)

    def shift(x, by):
        return lax.ppermute(x, "row", [(i, (i + by) % n_row) for i in range(n_row)])

    def shift_z(x, by):
        return lax.ppermute(
            x, "col", [(2 * z + c, 2 * ((z + by) % n_z) + c) for z in range(n_z) for c in range(2)])

    def swap(x):
        return lax.ppermute(x, "col", [(i, i ^ 1) for i in range(n_col)])

    dma = pltpu.SemaphoreType.DMA
    vmem = pl.BlockSpec(memory_space=pltpu.VMEM)
    hbm = pl.BlockSpec(memory_space=pltpu.HBM)
    anywhere = pl.BlockSpec(memory_space=pl.ANY)

    def in_hbm(x):
        return pltpu.with_memory_space_constraint(x, pltpu.HBM)

    def in_vmem(x):
        return pltpu.with_memory_space_constraint(x, pltpu.VMEM)

    outgoing, mine = pl.pallas_call(
        pick_kernel,
        in_specs=[hbm, hbm, hbm],
        out_specs=[vmem, vmem],
        out_shape=[arr(devices * 2 * SLOTS, lanes), jax.ShapeDtypeStruct((2, lanes), I32)],
        scratch_shapes=[pltpu.VMEM(owner.shape, I32), pltpu.VMEM(slot.shape, I32),
                        pltpu.VMEM(parent_solution.shape, F32), dma((3,))],
        compiler_params=pltpu.CompilerParams(vmem_limit_bytes=12 << 20),
        name="pick",
    )(in_hbm(owner), in_hbm(slot), in_hbm(parent_solution))
    received = lax.all_to_all(
        outgoing.reshape(devices, 2 * SLOTS, lanes), axes, split_axis=0, concat_axis=0, tiled=True)
    received = received.reshape(devices * 2 * SLOTS, lanes)
    inverse = pivot_inverse[0]
    placed = pl.pallas_call(
        place_kernel,
        in_specs=[vmem, vmem],
        out_specs=vmem,
        out_shape=arr(loads, block),
        compiler_params=pltpu.CompilerParams(vmem_limit_bytes=12 << 20),
        name="place",
    )(mine, received)
    tile, loaded = pl.pallas_call(
        load_kernel,
        in_specs=[anywhere, hbm],
        out_specs=[vmem, vmem],
        out_shape=[pltpu.VMEM(border_tile.shape[1:], F32), arr(8, lanes)],
        scratch_shapes=[dma((4,))],
        compiler_params=pltpu.CompilerParams(vmem_limit_bytes=4 << 20),
        cost_estimate=pl.CostEstimate(
            flops=0, transcendentals=0, bytes_accessed=8 * border_tile.shape[1] * border_tile.shape[2]),
        name="load",
    )(placed, in_hbm(border_tile[0]))
    def send_z(own):
        return {s: shift_z(own, s) for s in (2, 1, 3)}

    def held(kernel, name, scratch, out_shape, *args):
        return pl.pallas_call(
            kernel,
            in_specs=[vmem] * len(args),
            out_specs=jax.tree.map(lambda _: vmem, out_shape),
            out_shape=out_shape,
            scratch_shapes=scratch,
            compiler_params=pltpu.CompilerParams(vmem_limit_bytes=12 << 20),
            name=name,
        )(*args)

    def stack(got):
        return pl.pallas_call(
            stack_kernel,
            in_specs=[vmem] * n_z + [anywhere],
            out_specs=[vmem] * CHUNKS,
            out_shape=[arr(n_z, width, block)] * CHUNKS,
            compiler_params=pltpu.CompilerParams(vmem_limit_bytes=4 << 20),
            name="stack",
        )(placed, got[1], got[2], got[3], loaded)

    def begin(stacked):
        return held(begin_kernel, "begin", [pltpu.VMEM((2 * loads, n_z * block), BF16)],
                    arr(n_row, loads, quarter), in_vmem(tile), *stacked)

    def couple(begun, other, chunk):
        return held(functools.partial(couple_kernel, chunk=chunk), "couple",
                    [pltpu.VMEM((2 * width, n_z * block), BF16)],
                    [arr(width, quarter)] * n_row, in_vmem(tile), begun, other)

    def reduce(coupled, chunk):
        arrived = [shift(coupled[(s + 2) % 4], s) for s in (2, 1, 3)]
        return held(functools.partial(reduce_kernel, chunk=chunk), "reduce", [],
                    arr(quarter, width), rhs, coupled[2], *arrived)

    def spread(reduced):
        far, near, back = [shift(reduced, n_row - s) for s in (2, 1, 3)]
        return [reduced, near, far, back]

    def solve(pieces):
        scratch = [pltpu.VMEM((inverse.shape[1], 2 * width), BF16)]
        other = held(send_kernel, "send", scratch, arr(n_z, block, width), inverse, *pieces)
        return held(keep_kernel, "keep", scratch, [arr(block, width)] * n_z,
                    inverse, *pieces, swap(other))

    def finish(chip):
        got = [shift_z(chip[(s + 2) % 4], s) for s in (2, 1, 3)]
        return (chip[2] + got[0]) + (got[1] + got[2])

    chunks = range(CHUNKS)
    stacked = stack(send_z(placed))
    others = [swap(x) for x in stacked]
    begun = begin(stacked)
    coupled = [couple(begun, others[c], c) for c in chunks]
    reduced = [reduce(coupled[c], c) for c in chunks]
    pieces = [spread(reduced[c]) for c in chunks]
    chip = [solve(pieces[c]) for c in chunks]
    return jnp.concatenate([finish(chip[c]) for c in chunks], axis=1)[None]


def solution(mesh):
    return jax.shard_map(
        shards,
        mesh=mesh,
        in_specs=(
            P(("child", "row", "col"), None),
            P(),
            P(),
            P("child", "row", "col"),
            P("child", "row", "col"),
            P("child", "col", None),
        ),
        out_specs=P("child", ("row", "col"), None),
        check_vma=False,
    )
```

```python
import functools

import jax
import jax.numpy as jnp
from jax import lax
from jax.experimental import pallas as pl
from jax.experimental.pallas import tpu as pltpu
from jax.sharding import PartitionSpec as P

F32 = jnp.float32
BF16 = jnp.bfloat16
I32 = jnp.int32
CHUNKS = 2
SLOTS = 4


def position():
    col = lax.axis_index("col")
    return lax.axis_index(("child", "row", "col")), lax.axis_index("row"), col // 2, col % 2


def dot(a, b):
    return jnp.dot(a, b, preferred_element_type=F32)


def split2(x):
    hi = x.astype(BF16)
    return hi, (x - hi.astype(F32)).astype(BF16)


def split3(x):
    hi = x.astype(BF16)
    rest = x - hi.astype(F32)
    mid = rest.astype(BF16)
    return hi, mid, (rest - mid.astype(F32)).astype(BF16)


def ones_upto(n):
    rows = lax.broadcasted_iota(I32, (n, n), 0)
    cols = lax.broadcasted_iota(I32, (n, n), 1)
    return jnp.where(rows <= cols, 1.0, 0.0).astype(BF16)


def indicator(flag):
    return jnp.where(flag, 1.0, 0.0).astype(BF16)


def pick_kernel(owner_hbm, slot_hbm, parent_hbm, out_ref, mine_ref,
                owner_ref, slot_ref, parent_ref, sems):
    copies = [pltpu.make_async_copy(src, dst, sems.at[n]) for n, (src, dst) in enumerate(
        [(owner_hbm, owner_ref), (slot_hbm, slot_ref), (parent_hbm, parent_ref)])]
    for copy in copies:
        copy.start()
    copies[0].wait()
    me = position()[0]
    mine_ref[...] = owner_ref[pl.ds(2 * me, 2), :]
    blocks = owner_ref.shape[0] // 2
    lanes = owner_ref.shape[1]
    upto = ones_upto(lanes)
    copies[1].wait()
    copies[2].wait()
    parts = [split3(parent_ref[:, h * lanes:(h + 1) * lanes]) for h in range(2)]
    mask = [owner_ref[pl.ds(h, blocks, stride=2), :] == me for h in range(2)]
    slot = []
    children = 4
    per_child = blocks // children
    for h in range(2):
        slot.append(jnp.concatenate(
            [slot_ref[pl.ds(children * h + c, per_child, stride=2 * children), :]
             for c in range(children)], axis=0))
    count0 = dot(indicator(mask[0]), upto)
    count1 = dot(indicator(mask[1]), upto) + count0[:, lanes - 1:lanes]
    count = [count0, count1]
    local = lax.broadcasted_iota(I32, (blocks, lanes), 1)
    for p in range(SLOTS):
        asked = jnp.zeros((blocks, 1), I32)
        for h in range(2):
            chosen = mask[h] & (count[h] == float(p + 1))
            asked = asked + jnp.sum(jnp.where(chosen, slot[h] + 1, 0), axis=1, keepdims=True)
        select = indicator(local + 1 == asked)
        for h in range(2):
            hi, mid, lo = parts[h]
            out_ref[pl.ds(2 * p + h, blocks, stride=2 * SLOTS), :] = (
                dot(select, lo) + dot(select, mid)) + dot(select, hi)


def load_kernel(order_ref, tile_hbm, tile_ref, done_ref, sems):
    del order_ref
    done_ref[...] = jnp.zeros(done_ref.shape, F32)
    parts = sems.shape[0]
    rows = tile_ref.shape[0] // parts
    copies = []
    for n in range(parts):
        part = pl.ds(n * rows, rows)
        copies.append(pltpu.make_async_copy(tile_hbm.at[part], tile_ref.at[part], sems.at[n]))
    for copy in copies:
        copy.start()
    for copy in copies:
        copy.wait()


def place_kernel(mine_ref, got_ref, out_ref):
    lanes = mine_ref.shape[1]
    devices = got_ref.shape[0] // (2 * SLOTS)
    upto = ones_upto(lanes)
    source = lax.broadcasted_iota(I32, (devices, lanes), 0)
    flag = [source == mine_ref[h:h + 1, :] for h in range(2)]
    count0 = dot(indicator(flag[0]), upto)
    count1 = dot(indicator(flag[1]), upto) + count0[:, lanes - 1:lanes]
    count = [count0, count1]
    for half in range(2):
        acc = [jnp.zeros((lanes, lanes), F32) for _ in range(2)]
        for p in range(SLOTS):
            rows = got_ref[pl.ds(2 * p + half, devices, stride=2 * SLOTS), :]
            parts = split2(rows.T)
            for h in range(2):
                choose = indicator(flag[h] & (count[h] == float(p + 1)))
                for part in parts:
                    acc[h] = acc[h] + dot(part, choose)
        for h in range(2):
            out_ref[half * lanes:(half + 1) * lanes, h * lanes:(h + 1) * lanes] = acc[h]


def stack_kernel(a_ref, b_ref, c_ref, d_ref, order_ref, *outs):
    del order_ref
    width = outs[0].shape[1]
    for n, ref in enumerate((a_ref, b_ref, c_ref, d_ref)):
        for chunk, out in enumerate(outs):
            out[n] = ref[chunk * width:(chunk + 1) * width, :]


def block_rows(tile_ref, parity, first, cols, rows):
    _, _, z, core = position()
    parts = []
    for s in range(4):
        start = pl.multiple_of((2 * ((z + 4 - s) % 4) + (core + parity) % 2) * rows, rows)
        parts.append(tile_ref[pl.ds(start, rows), pl.ds(first, cols)])
    return jnp.concatenate(parts, axis=0)


def split_values(ref, split_ref, top, loads):
    n, width, rows = ref.shape
    for s in range(n):
        vh, vl = split2(ref[s])
        split_ref[top:top + width, s * rows:(s + 1) * rows] = vh
        split_ref[loads + top:loads + top + width, s * rows:(s + 1) * rows] = vl


def begin_kernel(tile_ref, a_ref, b_ref, out_ref, split_ref):
    width, rows = a_ref.shape[1:]
    loads = 2 * width
    split_values(a_ref, split_ref, 0, loads)
    split_values(b_ref, split_ref, width, loads)
    cols = out_ref.shape[2]
    for q in range(out_ref.shape[0]):
        th, tl = split2(block_rows(tile_ref, 0, q * cols, cols, rows))
        both = dot(split_ref[...], th)
        out_ref[q] = both[:loads] + (both[loads:] + dot(split_ref[:loads], tl))


def couple_kernel(tile_ref, sum_ref, other_ref, *rest, chunk):
    outs, split_ref = rest[:-1], rest[-1]
    row = position()[1]
    width, cols = outs[0].shape
    rows = other_ref.shape[2]
    split_values(other_ref, split_ref, 0, width)
    for s, out in enumerate(outs):
        q = (row + 2 + s) % 4
        th, tl = split2(block_rows(tile_ref, 1, pl.multiple_of(q * cols, cols), cols, rows))
        both = dot(split_ref[...], th)
        out[...] = sum_ref[q, chunk * width:(chunk + 1) * width, :] + (
            both[:width] + (both[width:] + dot(split_ref[:width], tl)))


def reduce_kernel(rhs_ref, a_ref, b_ref, c_ref, d_ref, out_ref, *, chunk):
    rows, width = out_ref.shape
    start = pl.multiple_of(position()[1] * rows, rows)
    total = (a_ref[...] + b_ref[...]) + (c_ref[...] + d_ref[...])
    out_ref[...] = rhs_ref[pl.ds(start, rows), chunk * width:(chunk + 1) * width] - total.T


def product(inv_ref, split_ref, parity, s):
    rows, width = 256, split_ref.shape[1] // 2
    _, _, z, core = position()
    start = pl.multiple_of((2 * ((z + 2 + s) % 4) + (core + parity) % 2) * rows, rows)
    ih, il = split2(inv_ref[pl.ds(start, rows), :])
    both = dot(ih, split_ref[...])
    return both[:, :width] + (both[:, width:] + dot(il, split_ref[:, :width]))


def split_pieces(refs, split_ref):
    row = position()[1]
    for s, ref in enumerate(refs):
        q, width = ref.shape
        start = pl.multiple_of(((row + s) % 4) * q, q)
        rh, rl = split2(ref[...])
        split_ref[pl.ds(start, q), :width] = rh
        split_ref[pl.ds(start, q), width:] = rl


def send_kernel(inv_ref, a_ref, b_ref, c_ref, d_ref, out_ref, split_ref):
    split_pieces((a_ref, b_ref, c_ref, d_ref), split_ref)
    for s in range(4):
        out_ref[s] = product(inv_ref, split_ref, 1, s)


def keep_kernel(inv_ref, a_ref, b_ref, c_ref, d_ref, add_ref, *rest):
    outs, split_ref = rest[:-1], rest[-1]
    split_pieces((a_ref, b_ref, c_ref, d_ref), split_ref)
    for s, out in enumerate(outs):
        out[...] = product(inv_ref, split_ref, 0, s) + add_ref[s]


def shards(parent_solution, border_owner, border_slot, border_tile, pivot_inverse, pivot_rhs):
    axes = ("child", "row", "col")
    n_child = lax.axis_size("child")
    n_row = lax.axis_size("row")
    n_col = lax.axis_size("col")
    n_z = n_col // 2
    devices = n_child * n_row * n_col
    rhs = pivot_rhs[0]
    loads = parent_solution.shape[1]
    lanes = 128
    width = loads // CHUNKS
    border = border_slot.shape[1]
    block = border // (n_row * n_col)
    quarter = rhs.shape[0] // n_row
    owner = border_owner.reshape(n_child * border // lanes, lanes)
    slot = border_slot.reshape(n_child, border // lanes, lanes).transpose(1, 0, 2).reshape(
        n_child * border // lanes, lanes)
    def arr(*shape):
        return jax.ShapeDtypeStruct(shape, F32)

    def shift(x, by):
        return lax.ppermute(x, "row", [(i, (i + by) % n_row) for i in range(n_row)])

    def shift_z(x, by):
        return lax.ppermute(
            x, "col", [(2 * z + c, 2 * ((z + by) % n_z) + c) for z in range(n_z) for c in range(2)])

    def swap(x):
        return lax.ppermute(x, "col", [(i, i ^ 1) for i in range(n_col)])

    dma = pltpu.SemaphoreType.DMA
    vmem = pl.BlockSpec(memory_space=pltpu.VMEM)
    hbm = pl.BlockSpec(memory_space=pltpu.HBM)
    anywhere = pl.BlockSpec(memory_space=pl.ANY)

    def in_hbm(x):
        return pltpu.with_memory_space_constraint(x, pltpu.HBM)

    def in_vmem(x):
        return pltpu.with_memory_space_constraint(x, pltpu.VMEM)

    outgoing, mine = pl.pallas_call(
        pick_kernel,
        in_specs=[hbm, hbm, hbm],
        out_specs=[vmem, vmem],
        out_shape=[arr(devices * 2 * SLOTS, lanes), jax.ShapeDtypeStruct((2, lanes), I32)],
        scratch_shapes=[pltpu.VMEM(owner.shape, I32), pltpu.VMEM(slot.shape, I32),
                        pltpu.VMEM(parent_solution.shape, F32), dma((3,))],
        compiler_params=pltpu.CompilerParams(vmem_limit_bytes=12 << 20),
        name="pick",
    )(in_hbm(owner), in_hbm(slot), in_hbm(parent_solution))
    received = lax.all_to_all(
        outgoing.reshape(devices, 2 * SLOTS, lanes), axes, split_axis=0, concat_axis=0, tiled=True)
    received = received.reshape(devices * 2 * SLOTS, lanes)
    inverse = pivot_inverse[0]
    placed = pl.pallas_call(
        place_kernel,
        in_specs=[vmem, vmem],
        out_specs=vmem,
        out_shape=arr(loads, block),
        compiler_params=pltpu.CompilerParams(vmem_limit_bytes=12 << 20),
        name="place",
    )(mine, received)
    tile, loaded = pl.pallas_call(
        load_kernel,
        in_specs=[anywhere, hbm],
        out_specs=[vmem, vmem],
        out_shape=[pltpu.VMEM(border_tile.shape[1:], F32), arr(8, lanes)],
        scratch_shapes=[dma((4,))],
        compiler_params=pltpu.CompilerParams(vmem_limit_bytes=4 << 20),
        cost_estimate=pl.CostEstimate(
            flops=0, transcendentals=0, bytes_accessed=8 * border_tile.shape[1] * border_tile.shape[2]),
        name="load",
    )(placed, in_hbm(border_tile[0]))
    def send_z(own):
        return {s: shift_z(own, s) for s in (3, 1, 2)}

    def held(kernel, name, scratch, out_shape, *args):
        return pl.pallas_call(
            kernel,
            in_specs=[vmem] * len(args),
            out_specs=jax.tree.map(lambda _: vmem, out_shape),
            out_shape=out_shape,
            scratch_shapes=scratch,
            compiler_params=pltpu.CompilerParams(vmem_limit_bytes=12 << 20),
            name=name,
        )(*args)

    def stack(got):
        return pl.pallas_call(
            stack_kernel,
            in_specs=[vmem] * n_z + [anywhere],
            out_specs=[vmem] * CHUNKS,
            out_shape=[arr(n_z, width, block)] * CHUNKS,
            compiler_params=pltpu.CompilerParams(vmem_limit_bytes=4 << 20),
            name="stack",
        )(placed, got[1], got[2], got[3], loaded)

    def begin(stacked):
        return held(begin_kernel, "begin", [pltpu.VMEM((2 * loads, n_z * block), BF16)],
                    arr(n_row, loads, quarter), in_vmem(tile), *stacked)

    def couple(begun, other, chunk):
        return held(functools.partial(couple_kernel, chunk=chunk), "couple",
                    [pltpu.VMEM((2 * width, n_z * block), BF16)],
                    [arr(width, quarter)] * n_row, in_vmem(tile), begun, other)

    def reduce(coupled, chunk):
        arrived = [shift(coupled[(s + 2) % 4], s) for s in (3, 1, 2)]
        return held(functools.partial(reduce_kernel, chunk=chunk), "reduce", [],
                    arr(quarter, width), rhs, coupled[2], *arrived)

    def spread(reduced):
        back, near, far = [shift(reduced, n_row - s) for s in (3, 1, 2)]
        return [reduced, near, far, back]

    def solve(pieces):
        scratch = [pltpu.VMEM((inverse.shape[1], 2 * width), BF16)]
        other = held(send_kernel, "send", scratch, arr(n_z, block, width), inverse, *pieces)
        return held(keep_kernel, "keep", scratch, [arr(block, width)] * n_z,
                    inverse, *pieces, swap(other))

    def finish(chip):
        got = [shift_z(chip[(s + 2) % 4], s) for s in (3, 1, 2)]
        return (chip[2] + got[0]) + (got[1] + got[2])

    chunks = range(CHUNKS)
    stacked = stack(send_z(placed))
    others = [swap(x) for x in stacked]
    begun = begin(stacked)
    coupled = [couple(begun, others[c], c) for c in chunks]
    reduced = [reduce(coupled[c], c) for c in chunks]
    pieces = [spread(reduced[c]) for c in chunks]
    chip = [solve(pieces[c]) for c in chunks]
    return jnp.concatenate([finish(chip[c]) for c in chunks], axis=1)[None]


def solution(mesh):
    return jax.shard_map(
        shards,
        mesh=mesh,
        in_specs=(
            P(("child", "row", "col"), None),
            P(),
            P(),
            P("child", "row", "col"),
            P("child", "row", "col"),
            P("child", "col", None),
        ),
        out_specs=P("child", ("row", "col"), None),
        check_vma=False,
    )
```
